32 devices in a mesh: groups: 2 (over x), ep: 16 (over z, y, core).
Axes of the slice: x: 2, y: 2, z: 4, core: 2. Of those that a mesh axis runs over, the one named last changes fastest.
Arguments:
- residual: bfloat16 [2048, 7168], P('groups', 'ep'), parts along dimension 0, may hold values from -6 to 6
- attn_out: bfloat16 [2048, 7168], P('groups', 'ep'), parts along dimension 0, may hold values from -6 to 6
- norm_gain: float32 [7168], replicated, may hold values from 0.5 to 1.5
- expert_routes: int32 [2048, 2], P(('groups', 'ep')), parts along dimension 0, may hold values from 0 to 2, as said below
- route_gain: float32 [2048, 2], P(('groups', 'ep')), parts along dimension 0, may hold values from 0.1 to 1
- w_gate: bfloat16 [7168, 4096], P(None, 'ep'), may hold values from -0.0625 to 0.0625
- w_up: bfloat16 [7168, 4096], P(None, 'ep'), may hold values from -0.0625 to 0.0625
- w_down: bfloat16 [4096, 7168], P('ep'), may hold values from -0.125 to 0.125
Outputs:
- mixed: bfloat16 [2048, 7168], P(('groups', 'ep')), parts along dimension 0
The draws below stay inside these ranges and needn't reach their ends.
There are 2 independent parts, one for each index of `groups`. The reference program is written for one: setup_inputs(seed, part) draws one part's arguments, and reference() takes and returns one part's arrays. A program takes and returns all parts, laid end to end along the dimension named above; an argument that names none is the same for every part. Nothing has to cross between parts.
Inputs may be any that keep to these rules, and one draw needn't show every extreme that they name: `expert_routes`: value 2 marks a route to an expert outside this wave; a token names each expert of the wave at most once. Among the tokens of one block of 64, at most 64 routes name one expert, and in every draw some expert is named exactly 64 times by every block.
All inputs are finite; a program needn't handle non-finite values.
Results may differ from the reference program's by a relative error of at most 0.0055.
Values may be sent and summed in bfloat16 or wider, within the bound.
A program may use at most 192 MiB of HBM per device.

```python
import math
import jax
import jax.numpy as jnp
from jax import lax

D = 7168
FF = 2048
FSPLIT = 8
TOK_DEV = 64
EW = 2
WSLOT = 2
CAP = 64
FF_DEV = 256
TOKENS = 1024


def draw_expert_routes(key, part):
    base = jax.random.fold_in(key, 7)
    key_perm, key_hot, key_coin = jax.random.split(base, 3)
    blocks = TOKENS // TOK_DEV
    perm_keys = jax.random.split(key_perm, blocks)
    orders = jax.vmap(lambda single: jax.random.permutation(single, EW))(perm_keys)
    position = (jnp.arange(TOK_DEV)[:, None] + jnp.arange(WSLOT)[None, :]) % EW
    named = orders[:, position]
    hottest = jax.random.randint(key_hot, (), 0, EW)
    coin_flip = jax.random.randint(key_coin, (blocks, TOK_DEV, WSLOT), 0, 2)
    live_mask = (coin_flip == 1) | (named == hottest)
    return jnp.where(live_mask, named, EW).reshape(TOKENS, WSLOT).astype(jnp.int32)


def level_of(key, shape, shards, smallest, largest):
    level = 1.0
    for dim, blocks in shards:
        steps = jax.random.uniform(jax.random.fold_in(jax.random.fold_in(key, 6), dim), (blocks,), jnp.float32, smallest / len(shards), largest / len(shards))
        level = level * jnp.repeat(jnp.exp(steps), shape[dim] // blocks).reshape((-1,) + (1,) * (len(shape) - 1 - dim))
    return level


def bell_draw(key, dims, scale, most, shards=(), kind=jnp.bfloat16):
    result = scale * jax.random.normal(key, dims, jnp.float32)
    if shards:
        result = result * level_of(key, dims, shards, -0.22, 0.18)
    return jnp.clip(result, -most, most).astype(kind)


def setup_inputs(seed: int = 0, part: int = 0) -> dict:
    splits = jax.random.split(jax.random.key(seed), 9)
    own_keys = jax.random.split(jax.random.fold_in(splits[8], part), 9)
    return {
        "residual": bell_draw(own_keys[0], (TOKENS, D), 1.0, 6.0, ((1, 16),)),
        "attn_out": bell_draw(own_keys[1], (TOKENS, D), 1.0, 6.0, ((1, 16),)),
        "norm_gain": jnp.clip(1.0 + 0.1 * jax.random.normal(splits[2], (D,), jnp.float32), 0.5, 1.5),
        "expert_routes": draw_expert_routes(jax.random.fold_in(jax.random.fold_in(splits[8], part), 71), part),
        "route_gain": jnp.clip(jnp.exp(math.log(1.0) - 2.3025851 * jax.random.uniform(own_keys[4], (TOKENS, WSLOT), jnp.float32) ** level_of(own_keys[4], (TOKENS, WSLOT), ((0, 16),), -0.2, 0.2)), 0.1, 1.0),
        "w_gate": bell_draw(splits[5], (D, EW * FF), D ** -0.5, 0.0625, ((1, 16),)),
        "w_up": bell_draw(splits[6], (D, EW * FF), D ** -0.5, 0.0625, ((1, 16),)),
        "w_down": bell_draw(splits[7], (EW * FF, D), FF ** -0.5, 0.125, ((0, 16),)),
    }


epsilon = 1e-06

def reference(residual, attn_out, norm_gain, expert_routes, route_gain, w_gate, w_up, w_down):
    stream = (residual.astype(jnp.float32) + attn_out.astype(jnp.float32)).astype(jnp.bfloat16)
    values = stream.astype(jnp.float32)
    inv_rms = lax.rsqrt(lax.optimization_barrier(jnp.mean(values * values, axis=-1, keepdims=True)) + epsilon)
    normed = (values * inv_rms * norm_gain).astype(jnp.bfloat16)
    blocks = TOKENS // TOK_DEV
    route_width = TOK_DEV * WSLOT
    route_ids = expert_routes.reshape(blocks, route_width)
    onehot = (route_ids[:, :, None] == jnp.arange(EW, dtype=jnp.int32)[None, None, :]).astype(jnp.int32)
    earlier = jnp.cumsum(onehot, axis=1) - onehot
    slot_pos = lax.optimization_barrier(jnp.sum(earlier * onehot, axis=2)).astype(jnp.int32)
    live_mask = route_ids < EW
    source = jnp.broadcast_to(jnp.arange(blocks, dtype=jnp.int32)[:, None], (blocks, route_width))
    token_index = (source * TOK_DEV + jnp.arange(route_width, dtype=jnp.int32)[None, :] // WSLOT).astype(jnp.int32)
    buffers = jnp.zeros((EW, blocks, CAP, D), jnp.bfloat16)
    buffers = buffers.at[route_ids, source, slot_pos].set(normed[token_index], mode='drop')

    def one_expert(expert_index):
        slot_rows = buffers[expert_index].reshape(blocks * CAP, D)
        column = (expert_index * FF).astype(jnp.int32)
        gate_cols = lax.dynamic_slice_in_dim(w_gate, column, FF, 1)
        up_cols = lax.dynamic_slice_in_dim(w_up, column, FF, 1)
        down_rows = lax.dynamic_slice_in_dim(w_down, column, FF, 0)
        gate_act = jnp.dot(slot_rows, gate_cols, preferred_element_type=jnp.float32)
        up_act = jnp.dot(slot_rows, up_cols, preferred_element_type=jnp.float32)
        hidden = (jax.nn.silu(gate_act) * up_act).astype(jnp.bfloat16)
        partials = jnp.einsum('rjh,jhd->jrd', hidden.reshape(blocks * CAP, FSPLIT, FF_DEV).astype(jnp.float32), down_rows.reshape(FSPLIT, FF_DEV, D).astype(jnp.float32), precision=lax.Precision.HIGHEST)
        rounded = lax.optimization_barrier(partials.astype(jnp.bfloat16))
        return lax.optimization_barrier(jnp.sum(rounded.astype(jnp.float32), axis=0))
    combined = lax.map(one_expert, jnp.arange(EW, dtype=jnp.int32))
    flat_rows = combined.reshape(EW * blocks * CAP, D)
    row_index = jnp.where(live_mask, route_ids * (blocks * CAP) + source * CAP + slot_pos, 0).astype(jnp.int32)
    live_gains = jnp.where(live_mask, route_gain.reshape(blocks, route_width), 0.0)
    picked = flat_rows[row_index] * live_gains[:, :, None]
    routed_sum = lax.optimization_barrier(jnp.sum(picked.reshape(TOKENS, WSLOT, D), axis=1))
    return (values + routed_sum).astype(jnp.bfloat16)
```

```python
import jax
import jax.numpy as jnp
from jax import lax
from jax.sharding import PartitionSpec as P

FSPLIT = 8


epsilon = 1e-06


def normalize(stream_rows, norm_gain):
    values = stream_rows.astype(jnp.float32)
    inv_rms = lax.rsqrt(jnp.mean(values * values, axis=-1, keepdims=True) + epsilon)
    return (values * inv_rms * norm_gain).astype(jnp.bfloat16)


def route_match(routes, experts, capacity):
    flat_ids = routes.reshape(-1)
    onehot = (flat_ids[:, None] == jnp.arange(experts, dtype=jnp.int32)[None, :]).astype(jnp.int32)
    earlier = jnp.cumsum(onehot, axis=0) - onehot
    slot_pos = jnp.sum(earlier * onehot, axis=1)
    slot_code = jnp.where(flat_ids < experts, flat_ids * capacity + slot_pos, -1)
    target = jnp.arange(experts * capacity, dtype=jnp.int32)
    return slot_code[None, :] == target[:, None]


def selection(routes, experts, capacity):
    matched = route_match(routes, experts, capacity).astype(jnp.int32)
    return matched.reshape(experts * capacity, routes.shape[0], routes.shape[1]).sum(axis=2)


def gain_table(routes, route_gain, experts, capacity):
    matched = route_match(routes, experts, capacity)
    weighted = jnp.where(matched, route_gain.reshape(-1)[None, :], 0.0)
    return weighted.reshape(experts * capacity, routes.shape[0], routes.shape[1]).sum(axis=2).T


def expert_rows(normed, w_gate, w_up, w_down):
    gate_act = jnp.dot(normed, w_gate, preferred_element_type=jnp.float32)
    up_act = jnp.dot(normed, w_up, preferred_element_type=jnp.float32)
    hidden = (jax.nn.silu(gate_act) * up_act).astype(jnp.bfloat16)
    return jnp.dot(hidden, w_down, preferred_element_type=jnp.float32).astype(jnp.bfloat16)


def body(residual, attn_out, norm_gain, expert_routes, route_gain, w_gate, w_up, w_down):
    devices = lax.axis_size("ep")
    tok_here = expert_routes.shape[0]
    route_slots = expert_routes.shape[1]
    experts = devices // FSPLIT
    capacity = route_slots * tok_here // experts
    model_width = w_gate.shape[0]
    stream_feat = (residual.astype(jnp.float32) + attn_out.astype(jnp.float32)).astype(jnp.bfloat16)
    stream_rows = lax.all_to_all(stream_feat, "ep", split_axis=0, concat_axis=1, tiled=True)
    combine_weights = gain_table(expert_routes, route_gain, experts, capacity)
    normed_rows = normalize(stream_rows, norm_gain)
    select = selection(expert_routes, experts, capacity).astype(jnp.bfloat16)
    per_expert = jnp.dot(select, normed_rows, preferred_element_type=jnp.float32).astype(
        jnp.bfloat16
    )
    per_expert = per_expert.reshape(experts, 1, capacity, model_width)
    outgoing = jnp.broadcast_to(per_expert, (experts, FSPLIT, capacity, model_width))
    outgoing = outgoing.reshape(devices, capacity, model_width)
    received = lax.all_to_all(outgoing, "ep", split_axis=0, concat_axis=0, tiled=True)
    slot_count = received.shape[1]
    partial_value = expert_rows(received.reshape(-1, model_width), w_gate, w_up, w_down)
    partial_value = partial_value.reshape(devices, slot_count, model_width)
    returned = lax.all_to_all(partial_value, "ep", split_axis=0, concat_axis=0, tiled=True)
    summed = (
        returned.reshape(experts, FSPLIT, capacity, model_width).astype(jnp.float32).sum(axis=1)
    )
    summed = summed.reshape(experts * capacity, model_width)
    routed_sum = jnp.dot(combine_weights, summed, precision=lax.Precision.HIGHEST)
    return (stream_rows.astype(jnp.float32) + routed_sum).astype(jnp.bfloat16)


def dense_body(residual, attn_out, norm_gain, expert_routes, route_gain, w_gate, w_up, w_down):
    devices = lax.axis_size("ep")
    rank = lax.axis_index("ep")
    tok_here = expert_routes.shape[0]
    experts = devices // FSPLIT
    stream_feat = (residual.astype(jnp.float32) + attn_out.astype(jnp.float32)).astype(jnp.bfloat16)
    named = jnp.arange(experts, dtype=jnp.int32)
    gains = jnp.sum(
        jnp.where(expert_routes[:, :, None] == named, route_gain[:, :, None], 0.0), axis=1
    )
    all_gains = lax.all_gather(gains, "ep", axis=0, tiled=True)
    here = (rank // FSPLIT == named).astype(jnp.float32)
    gain_here = jnp.sum(all_gains * here, axis=1, keepdims=True)
    stream = lax.all_gather(stream_feat, "ep", axis=1, tiled=True)
    normed = normalize(stream, norm_gain)
    gate_act = jnp.dot(normed, w_gate, preferred_element_type=jnp.float32)
    up_act = jnp.dot(normed, w_up, preferred_element_type=jnp.float32)
    hidden = (jax.nn.silu(gate_act) * up_act * gain_here).astype(jnp.bfloat16)
    partial = jnp.dot(hidden, w_down, preferred_element_type=jnp.float32).astype(jnp.bfloat16)
    routed = lax.psum_scatter(partial, "ep", scatter_dimension=0, tiled=True)
    own = lax.dynamic_slice_in_dim(stream, rank * tok_here, tok_here, 0)
    return (own.astype(jnp.float32) + routed.astype(jnp.float32)).astype(jnp.bfloat16)


def pick_body(residual, attn_out, norm_gain, expert_routes, route_gain, w_gate, w_up, w_down):
    experts = lax.axis_size("ep") // FSPLIT
    capacity = expert_routes.shape[1] * expert_routes.shape[0] // experts
    run = dense_body if capacity >= expert_routes.shape[0] else body
    return run(residual, attn_out, norm_gain, expert_routes, route_gain, w_gate, w_up, w_down)


def solution(mesh):
    in_specs = (
        P("groups", "ep"),
        P("groups", "ep"),
        P(),
        P(("groups", "ep"), None),
        P(("groups", "ep"), None),
        P(None, "ep"),
        P(None, "ep"),
        P("ep", None),
    )
    out_specs = P(("groups", "ep"), None)
    return jax.shard_map(pick_body, mesh=mesh, in_specs=in_specs, out_specs=out_specs, check_vma=False)
```
